32 devices in a mesh: lat: 8 (over z, y), lay: 4 (over x, core).
Axes of the slice: x: 2, y: 2, z: 4, core: 2. Of those that a mesh axis runs over, the one named last changes fastest.
Arguments:
- wave_field: float32 [2, 32, 512, 512], P(None, 'lay', 'lat'), may hold values from -6 to 6
- contrast: float32 [32, 512, 512], P('lay', 'lat'), may hold values from 0.1 to 1.5
- layer_of_plane: int32 [32], replicated, may hold values from 0 to 7, never falling along the last dimension, each value on 1 to 8 neighbouring positions
- toeplitz_table: float32 [2, 8, 63], replicated, may hold values from -1 to 1
- hankel_table: float32 [2, 8, 63], replicated, may hold values from -1 to 1
- layer_rates: float32 [8], replicated, may hold values from 0.5 to 1.5
Outputs:
- scattered_field: float32 [2, 32, 512, 512], P(None, 'lay', 'lat')
The draws below stay inside these ranges and needn't reach their ends.
Inputs may be any that keep to these rules, and one draw needn't show every extreme that they name: `layer_of_plane`: layer numbers never fall from one plane to the next; every layer holds 1 to 8 planes.
All inputs are finite; a program needn't handle non-finite values.
Results may differ from the reference program's by a relative error of at most 0.00007.
Values sent between devices are 32-bit elements; how exact they have to be, the bound alone decides.
A program may use at most 128 MiB of HBM per device.

```python
import math
import jax
import jax.numpy as jnp
import numpy as np
from jax import lax

NX = 512
NY = 512
LAYERS = 8
NZ = 32


def steps_of(key, shape, cuts, least, largest):
    factor_of, own = 1.0, jax.random.fold_in(key, 6)
    for position, parts in cuts:
        steps = jnp.exp(jax.random.uniform(jax.random.fold_in(own, position), (parts,), jnp.float32, least / len(cuts), largest / len(cuts)))
        factor_of = factor_of * jnp.repeat(steps, shape[position] // parts).reshape([-1 if axis == position else 1 for axis in range(len(shape))])
    return factor_of


def profile(count, total, reach, skew):
    portions = [(1 << 20) // math.isqrt(rank ** skew) + 1 for rank in range(2, count + 1)]
    surplus, given = total - reach - (count - 1), [1] * (count - 1)
    while surplus > 0:
        movable = [i for i in range(count - 1) if given[i] < reach]
        mass, left = sum([portions[i] for i in movable]), surplus
        for i in movable:
            extra = min(reach - given[i], max(1, left * portions[i] // mass), surplus)
            given[i] = given[i] + extra
            surplus = surplus - extra
    return np.array([reach] + given)


def uneven_parts(own_key, number_of, total, most, slope):
    if number_of == 2:
        one = jax.random.randint(own_key, (), max(1, total - most), min(most, total - 1) + 1)
        return jnp.stack([one, total - one])
    lengths = jnp.asarray(profile(number_of, total, most, slope), jnp.int32)
    twos = (number_of - 1) // 2
    giver, taker = lengths[1:1 + 2 * twos:2], lengths[2:2 + 2 * twos:2]
    margin = jnp.minimum(giver - 1, most - taker)
    shifted = jax.random.randint(jax.random.fold_in(own_key, 1), (twos,), 0, 1 << 20) % (margin + 1)
    lengths = lengths.at[1:1 + 2 * twos:2].set(giver - shifted).at[2:2 + 2 * twos:2].set(taker + shifted)
    return lengths[jax.random.permutation(jax.random.fold_in(own_key, 2), number_of)]


def noise(key, shape, scale, reach, pieces=(), dtype=jnp.bfloat16):
    factor_of = steps_of(key, shape, pieces, -0.22, 0.18) if pieces else 1.0
    array = jax.random.normal(key, shape, jnp.float32) * scale * factor_of
    return jnp.minimum(jnp.maximum(array, -reach), reach).astype(dtype)


def setup_inputs(seed: int = 0) -> dict:
    key_list = jax.random.split(jax.random.key(seed), 7)
    wave_field = noise(key_list[0], (2, NZ, NX, NY), 1.0, 6.0, ((1, 4), (2, 8)), jnp.float32)
    contrast = jnp.clip(0.1 + 1.4 * jax.random.uniform(key_list[1], (NZ, NX, NY), jnp.float32) ** steps_of(key_list[1], (NZ, NX, NY), ((0, 4), (1, 8)), -0.2, 0.2), 0.1, 1.5)
    layer_of_plane = jnp.searchsorted(jnp.cumsum(uneven_parts(key_list[2], LAYERS, NZ, 2 * NZ // LAYERS, 2)), jnp.arange(NZ), side="right").astype(jnp.int32)
    toeplitz_table = noise(key_list[3], (2, LAYERS, 2 * NZ - 1), NZ ** -0.5, 1.0, (), jnp.float32)
    hankel_table = noise(key_list[4], (2, LAYERS, 2 * NZ - 1), NZ ** -0.5, 1.0, (), jnp.float32)
    layer_rates = jnp.clip(jnp.exp(jax.random.uniform(key_list[5], (LAYERS,), jnp.float32, math.log(0.5), math.log(1.5))), 0.5, 1.5)
    return {"wave_field": wave_field, "contrast": contrast, "layer_of_plane": layer_of_plane, "toeplitz_table": toeplitz_table, "hankel_table": hankel_table, "layer_rates": layer_rates}


def signed_freq(amount):
    index = jnp.arange(amount).astype(jnp.int32)
    return jnp.where(index >= amount // 2, index - amount, index).astype(jnp.float32) / (amount / 2)

def reference(wave_field, contrast, layer_of_plane, toeplitz_table, hankel_table, layer_rates):
    complex_field = wave_field[0] + 1j * wave_field[1]
    spectrum = jnp.fft.fft2(complex_field, axes=(1, 2))
    freq_x = signed_freq(NX)
    freq_y = signed_freq(NY)
    steepness = jnp.sqrt(1.0 + freq_x[:, None] ** 2 + freq_y[None, :] ** 2)
    planes = jnp.arange(NZ).astype(jnp.int32)
    toeplitz_c = toeplitz_table[0] + 1j * toeplitz_table[1]
    hankel_c = hankel_table[0] + 1j * hankel_table[1]

    def one_plane(plane):
        layer_here = layer_of_plane[plane]
        rate_here = layer_rates[layer_here]
        offset = plane - planes
        amp_toeplitz = toeplitz_c[layer_here, offset + NZ - 1]
        amp_hankel = hankel_c[layer_here, plane + planes]
        decay_toeplitz = jnp.exp(-rate_here * steepness[None] * jnp.abs(offset).astype(jnp.float32)[:, None, None] / NZ)
        decay_hankel = jnp.exp(-rate_here * steepness[None] * (plane + planes).astype(jnp.float32)[:, None, None] / (2 * NZ))
        kernel = amp_toeplitz[:, None, None] * decay_toeplitz + amp_hankel[:, None, None] * decay_hankel
        return lax.optimization_barrier(jnp.sum(kernel * spectrum, axis=0))
    mixed = lax.map(one_plane, planes)
    space = jnp.fft.ifft2(mixed, axes=(1, 2))
    return jnp.stack([jnp.real(space) * contrast, jnp.imag(space) * contrast]).astype(jnp.float32)
```

```python
import math

import functools

import jax
import jax.numpy as jnp
import numpy as np
from jax import lax
from jax.experimental import pallas as pl
from jax.experimental.pallas import tpu as pltpu
from jax.sharding import PartitionSpec as P

HIGHEST = lax.Precision.HIGHEST


def signed_of(index, amount):
    return jnp.where(index >= amount // 2, index - amount, index).astype(jnp.float32) / (amount / 2)


def phase_tables(rows, cols, amount, sign):
    index_row = lax.broadcasted_iota(jnp.int32, (rows, cols), 0)
    index_col = lax.broadcasted_iota(jnp.int32, (rows, cols), 1)
    angle = 2.0 * math.pi / amount * (index_row * index_col % amount).astype(jnp.float32)
    return (jnp.cos(angle), sign * jnp.sin(angle))


def complex_apply(real_part, imag_part, cos_table, sin_table, form):
    out_real = jnp.einsum(form, real_part, cos_table, precision=HIGHEST) - jnp.einsum(
        form, imag_part, sin_table, precision=HIGHEST
    )
    out_imag = jnp.einsum(form, real_part, sin_table, precision=HIGHEST) + jnp.einsum(
        form, imag_part, cos_table, precision=HIGHEST
    )
    return (out_real, out_imag)


def fourier_last(real_part, imag_part, sign, factor):
    amount = real_part.shape[-1]
    leading = real_part.shape[:-1]
    first = 1
    for divisor in range(1, math.isqrt(amount) + 1):
        if amount % divisor == 0:
            first = divisor
    second = amount // first
    flat_real = real_part.reshape(-1, second, first)
    flat_imag = imag_part.reshape(-1, second, first)
    cos_second, sin_second = phase_tables(second, second, second, sign)
    section_real, section_imag = complex_apply(
        flat_real, flat_imag, cos_second, sin_second, "pmn,mk->pkn"
    )
    twist_cos, twist_sin = phase_tables(second, first, amount, sign)
    turned_real = section_real * twist_cos - section_imag * twist_sin
    turned_imag = section_real * twist_sin + section_imag * twist_cos
    cos_first, sin_first = phase_tables(first, first, first, sign)
    final_real, final_imag = complex_apply(
        turned_real, turned_imag, cos_first, sin_first, "pkn,nj->pjk"
    )
    final_real = final_real.reshape(leading + (amount,)) * factor
    final_imag = final_imag.reshape(leading + (amount,)) * factor
    return (final_real, final_imag)


def pick_amplitudes(rows, index, width):
    positions = jnp.arange(width, dtype=jnp.int32)
    onehot = (index[:, :, None] == positions[None, None, :]).astype(jnp.float32)
    return jnp.einsum("pan,ain->pai", rows, onehot, precision=HIGHEST)


def general_body(wave_field, contrast, layer_of_plane, toeplitz_table, hankel_table, layer_rates):
    row_count = wave_field.shape[2]
    width_y = wave_field.shape[3]
    lat_count = lax.axis_size("lat")
    lay_count = lax.axis_size("lay")
    width_x = row_count * lat_count
    ky_band = width_y // lat_count
    table_width = toeplitz_table.shape[-1]
    plane_total = (table_width + 1) // 2
    layer_count = layer_rates.shape[0]
    spec_real, spec_imag = fourier_last(wave_field[0], wave_field[1], -1.0, 1.0)
    along_y = jnp.stack([spec_real, spec_imag], 2)
    freq_x = signed_of(jnp.arange(width_x, dtype=jnp.int32), width_x)
    ky_first = lax.axis_index("lat") * ky_band
    layer_ids = jnp.arange(layer_count, dtype=jnp.int32)

    def couple(z_out, z_in, source, ky_rows):
        onehot = (layer_of_plane[z_out][:, None] == layer_ids[None, :]).astype(jnp.float32)
        rate_out = jnp.dot(onehot, layer_rates, precision=HIGHEST)
        rows_toeplitz = jnp.einsum("al,pln->pan", onehot, toeplitz_table, precision=HIGHEST)
        rows_hankel = jnp.einsum("al,pln->pan", onehot, hankel_table, precision=HIGHEST)
        offset = z_out[:, None] - z_in[None, :]
        plane_sum = z_out[:, None] + z_in[None, :]
        amp_toeplitz = pick_amplitudes(rows_toeplitz, offset + plane_total - 1, table_width)
        amp_hankel = pick_amplitudes(rows_hankel, plane_sum, table_width)
        freq_y = signed_of(ky_rows, width_y)
        steepness = jnp.sqrt(1.0 + freq_y[:, None] ** 2 + freq_x[None, :] ** 2)
        scaled = rate_out[:, None, None, None] * steepness[None, None] / plane_total
        decay_toeplitz = jnp.exp(-scaled * jnp.abs(offset).astype(jnp.float32)[:, :, None, None])
        decay_hankel = jnp.exp(-scaled * (0.5 * plane_sum.astype(jnp.float32))[:, :, None, None])
        kern_real = (
            amp_toeplitz[0][:, :, None, None] * decay_toeplitz
            + amp_hankel[0][:, :, None, None] * decay_hankel
        )
        kern_imag = (
            amp_toeplitz[1][:, :, None, None] * decay_toeplitz
            + amp_hankel[1][:, :, None, None] * decay_hankel
        )
        real_src = source[None, :, 0]
        imag_src = source[None, :, 1]
        out_real = jnp.sum(kern_real * real_src - kern_imag * imag_src, axis=1)
        out_imag = jnp.sum(kern_real * imag_src + kern_imag * real_src, axis=1)
        return jnp.stack([out_real, out_imag], 1)

    narrow = ky_band // lay_count
    narrow_rows = ky_first + lax.axis_index("lay") * narrow + jnp.arange(narrow, dtype=jnp.int32)
    lines_in = lax.all_to_all(along_y, "lat", split_axis=3, concat_axis=1, tiled=True)
    line_real = jnp.transpose(lines_in[:, :, 0], (0, 2, 1))
    line_imag = jnp.transpose(lines_in[:, :, 1], (0, 2, 1))
    out_real, out_imag = fourier_last(line_real, line_imag, -1.0, 1.0)
    spectrum = jnp.stack([out_real, out_imag], 1)
    gathered = lax.all_to_all(spectrum, "lay", split_axis=2, concat_axis=0, tiled=True)
    all_planes = gathered.shape[0]
    every_plane = jnp.arange(all_planes, dtype=jnp.int32)
    block_size = math.gcd(all_planes, 8)

    def one_block(which):
        z_out = which * block_size + jnp.arange(block_size, dtype=jnp.int32)
        return couple(z_out, every_plane, gathered, narrow_rows)

    stacked = lax.map(one_block, jnp.arange(all_planes // block_size, dtype=jnp.int32))
    coupled = stacked.reshape(all_planes, 2, narrow_rows.shape[0], width_x)
    mixed = lax.all_to_all(coupled, "lay", split_axis=0, concat_axis=2, tiled=True)
    out_real, out_imag = fourier_last(mixed[:, 0], mixed[:, 1], 1.0, 1.0 / width_x)
    spatial_x = jnp.transpose(jnp.stack([out_real, out_imag], 1), (0, 3, 1, 2))
    lines = lax.all_to_all(spatial_x, "lat", split_axis=1, concat_axis=3, tiled=True)
    space_real, space_imag = fourier_last(lines[:, :, 0], lines[:, :, 1], 1.0, 1.0 / width_y)
    return jnp.stack([space_real, space_imag], 0) * contrast[None]


LANES = 128
SUBLANES = 8
MESH = pl.DeviceIdType.MESH


def split_tables(amount):
    half = amount // 2
    index = np.arange(half)
    angle = 2.0 * np.pi / half * (index[:, None] * index[None, :] % half)
    cos_part, sin_part = np.cos(angle), np.sin(angle)
    right = np.block([[cos_part, -sin_part], [sin_part, cos_part]]).astype(np.float32)
    high = right.astype(jnp.bfloat16)
    low = (right - high.astype(np.float32)).astype(jnp.bfloat16)
    turn = 2.0 * np.pi / amount * index
    twiddle = np.stack([np.cos(turn), np.sin(turn)]).astype(np.float32)
    return high, low, np.ascontiguousarray(high.T), np.ascontiguousarray(low.T), twiddle


def split(value):
    high = value.astype(jnp.bfloat16)
    return high, (value - high.astype(jnp.float32)).astype(jnp.bfloat16)


def product(left, right, contract):
    dot = functools.partial(
        lax.dot_general,
        dimension_numbers=(contract, ((), ())),
        preferred_element_type=jnp.float32,
    )
    return dot(left[0], right[0]) + (dot(left[1], right[0]) + dot(left[0], right[1]))


def swap_halves(first, second):
    low = lax.broadcasted_iota(jnp.int32, first.shape, first.ndim - 1) < LANES // 2
    one = jnp.where(low, first, pltpu.roll(second, LANES // 2, first.ndim - 1))
    two = jnp.where(low, pltpu.roll(first, LANES // 2, first.ndim - 1), second)
    return one, two


def butterfly_in(real_part, imag_part, twiddle):
    half = real_part.shape[-1] // 2
    cos_row, sin_row = twiddle[0:1, :], twiddle[1:2, :]
    even = (real_part[:, :half] + real_part[:, half:], imag_part[:, :half] + imag_part[:, half:])
    real_gap = real_part[:, :half] - real_part[:, half:]
    imag_gap = imag_part[:, :half] - imag_part[:, half:]
    odd = (
        real_gap * cos_row + imag_gap * sin_row,
        imag_gap * cos_row - real_gap * sin_row,
    )
    return even, odd


def butterfly_out(even, odd, twiddle):
    cos_row, sin_row = twiddle[0:1, :], twiddle[1:2, :]
    real_turn = odd[0] * cos_row - odd[1] * sin_row
    imag_turn = odd[0] * sin_row + odd[1] * cos_row
    real_part = jnp.concatenate([even[0] + real_turn, even[0] - real_turn], 1)
    imag_part = jnp.concatenate([even[1] + imag_turn, even[1] - imag_turn], 1)
    return real_part, imag_part


def couple_kernel(
    lat_count, lay_count, planes, rows,
    layer_ref, rate_ref, toeplitz_ref, hankel_ref,
    field_ref, fh_ref, fl_ref, ih_ref, il_ref, twiddle_ref,
    out_ref,
    send_in, recv_in, send_out, field_x, spectrum, mixed, powers,
    send_sem, recv_sem,
):
    device_count = lat_count * lay_count
    my_lat, my_lay = lax.axis_index("lat"), lax.axis_index("lay")
    me = my_lat * lay_count + my_lay
    width_y = field_ref.shape[2]
    width_x = rows * lat_count
    half_y, half_x = width_y // 2, width_x // 2
    band = width_y // device_count
    parts = band // SUBLANES
    plane_total = planes * lay_count
    layer_count = rate_ref.shape[0]
    bands_half = device_count // 2

    def partner(step):
        to_lat = (my_lat + step // lay_count) % lat_count
        to_lay = (my_lay + step % lay_count) % lay_count
        return to_lat, to_lay

    barrier = pltpu.get_barrier_semaphore()

    def greet(step, carry):
        pl.semaphore_signal(barrier, inc=1, device_id=partner(step), device_id_type=MESH)
        return carry

    lax.fori_loop(1, device_count, greet, 0)

    def exchange(source, target, part, phase, step):
        to_lat, to_lay = partner(step)
        rows_part = pl.ds(part * SUBLANES, SUBLANES)
        return pltpu.make_async_remote_copy(
            src_ref=source.at[to_lat * lay_count + to_lay, :, rows_part, :],
            dst_ref=target.at[me, :, rows_part, :],
            send_sem=send_sem.at[phase, step],
            recv_sem=recv_sem.at[phase, step],
            device_id=(to_lat, to_lay),
            device_id_type=MESH,
        )

    def start_all(source, target, part, phase):
        def one(step, carry):
            exchange(source, target, part, phase, step).start()
            return carry

        lax.fori_loop(1, device_count, one, 0)
        rows_part = slice(part * SUBLANES, (part + 1) * SUBLANES)
        target[me, :, rows_part, :] = source[me, :, rows_part, :]

    def wait_recv(source, target, part, phase):
        def one(step, carry):
            exchange(source, target, part, phase, step).wait_recv()
            return carry

        lax.fori_loop(1, device_count, one, 0)

    def wait_send(source, target, part, phase):
        def one(step, carry):
            exchange(source, target, part, phase, step).wait_send()
            return carry

        lax.fori_loop(1, device_count, one, 0)

    lines = field_ref.shape[1]
    chunk = min(lines, 2 * LANES)
    for start in range(0, lines, chunk):
        where = slice(start, start + chunk)
        pairs = butterfly_in(field_ref[0, where, :], field_ref[1, where, :], twiddle_ref)
        for side, (real_part, imag_part) in enumerate(pairs):
            right = split(jnp.concatenate([real_part, imag_part], 1))
            result = product((ih_ref[...], il_ref[...]), right, ((1,), (1,)))
            for comp in range(2):
                piece = result[comp * half_y:(comp + 1) * half_y]
                send_in[side * bands_half:(side + 1) * bands_half, comp, :, where] = (
                    piece.reshape(bands_half, band, chunk)
                )

    pl.semaphore_wait(barrier, device_count - 1)
    for part in range(parts):
        start_all(send_in, recv_in, part, part)

    def signed(position, amount):
        index = 2 * (position % (amount // 2)) + position // (amount // 2)
        index = jnp.where(index >= amount // 2, index - amount, index)
        return index.astype(jnp.float32) / (amount / 2)

    tile = (SUBLANES, width_x)
    freq_x = signed(lax.broadcasted_iota(jnp.int32, tile, 1), width_x)
    for part in range(parts):
        ky = me * band + part * SUBLANES + lax.broadcasted_iota(jnp.int32, tile, 0)
        freq_y = signed(ky, width_y)
        steepness = jnp.sqrt(1.0 + freq_x * freq_x + freq_y * freq_y)

        def one_layer(layer, carry):
            base = jnp.exp(steepness * (-rate_ref[layer] / (2 * plane_total)))

            def one_power(m, value):
                powers[part, layer, m] = value
                return value * base

            lax.fori_loop(0, 2 * plane_total - 1, one_power, jnp.ones(tile, jnp.float32))
            return carry

        lax.fori_loop(0, layer_count, one_layer, 0)

    def load_lines(part):
        rows_part = slice(part * SUBLANES, (part + 1) * SUBLANES)

        def one_lay(lay, carry):
            for pair in range(planes // 2):
                lanes = slice(pair * LANES, (pair + 1) * LANES)
                for block in range(lat_count // 2):
                    first = recv_in[2 * block * lay_count + lay, :, rows_part, lanes]
                    second = recv_in[(2 * block + 1) * lay_count + lay, :, rows_part, lanes]
                    even, odd = swap_halves(first, second)
                    place = slice(block * LANES, (block + 1) * LANES)
                    field_x[:, lay * planes + 2 * pair, :, place] = even
                    field_x[:, lay * planes + 2 * pair + 1, :, place] = odd
            return carry

        lax.fori_loop(0, lay_count, one_lay, 0)

    def store_lines(part):
        rows_part = slice(part * SUBLANES, (part + 1) * SUBLANES)

        def one_lay(lay, carry):
            for pair in range(planes // 2):
                lanes = slice(pair * LANES, (pair + 1) * LANES)
                for block in range(lat_count // 2):
                    place = slice(block * LANES, (block + 1) * LANES)
                    even = field_x[:, lay * planes + 2 * pair, :, place]
                    odd = field_x[:, lay * planes + 2 * pair + 1, :, place]
                    first, second = swap_halves(even, odd)
                    send_out[2 * block * lay_count + lay, :, rows_part, lanes] = first
                    send_out[(2 * block + 1) * lay_count + lay, :, rows_part, lanes] = second
            return carry

        lax.fori_loop(0, lay_count, one_lay, 0)

    group = min(plane_total, LANES // SUBLANES)

    def transform_x(step, carry):
        some = pl.ds(step * group, group)
        flat = (group * SUBLANES, width_x)
        pairs = butterfly_in(
            field_x[0, some].reshape(flat), field_x[1, some].reshape(flat), twiddle_ref
        )
        for side, (real_part, imag_part) in enumerate(pairs):
            left = split(jnp.concatenate([real_part, imag_part], 1))
            result = product(left, (fh_ref[...], fl_ref[...]), ((1,), (0,)))
            for comp in range(2):
                piece = result[:, comp * half_x:(comp + 1) * half_x]
                spectrum[comp, some, :, side * half_x:(side + 1) * half_x] = piece.reshape(
                    group, SUBLANES, half_x
                )
        return carry

    def invert_x(step, carry):
        some = pl.ds(step * group, group)
        sides = []
        for side in range(2):
            place = slice(side * half_x, (side + 1) * half_x)
            flat = (group * SUBLANES, half_x)
            left = split(
                jnp.concatenate(
                    [mixed[0, some, :, place].reshape(flat), mixed[1, some, :, place].reshape(flat)], 1
                )
            )
            result = product(left, (ih_ref[...], il_ref[...]), ((1,), (0,)))
            sides.append((result[:, :half_x], result[:, half_x:]))
        real_part, imag_part = butterfly_out(sides[0], sides[1], twiddle_ref)
        full = (group, SUBLANES, width_x)
        field_x[0, some] = (real_part * (1.0 / width_x)).reshape(full)
        field_x[1, some] = (imag_part * (1.0 / width_x)).reshape(full)
        return carry

    def couple(part):
        def one_plane(plane, carry):
            layer = layer_ref[plane]
            real_sum = jnp.zeros(tile, jnp.float32)
            imag_sum = jnp.zeros(tile, jnp.float32)
            for source in range(plane_total):
                offset = plane - source
                direct = powers[part, layer, 2 * jnp.abs(offset)]
                mirror = powers[part, layer, plane + source]
                at = offset + plane_total - 1
                kern_real = (
                    toeplitz_ref[0, layer, at] * direct
                    + hankel_ref[0, layer, plane + source] * mirror
                )
                kern_imag = (
                    toeplitz_ref[1, layer, at] * direct
                    + hankel_ref[1, layer, plane + source] * mirror
                )
                real_src, imag_src = spectrum[0, source], spectrum[1, source]
                real_sum += kern_real * real_src - kern_imag * imag_src
                imag_sum += kern_real * imag_src + kern_imag * real_src
            mixed[0, plane] = real_sum
            mixed[1, plane] = imag_sum
            return carry

        lax.fori_loop(0, plane_total, one_plane, 0)

    for part in range(parts):
        wait_recv(send_in, recv_in, part, part)
        load_lines(part)
        lax.fori_loop(0, plane_total // group, transform_x, 0)
        couple(part)
        lax.fori_loop(0, plane_total // group, invert_x, 0)
        store_lines(part)
        start_all(send_out, out_ref, part, parts + part)
    for part in range(parts):
        wait_send(send_in, recv_in, part, part)
    for part in range(parts):
        wait_recv(send_out, out_ref, part, parts + part)
        wait_send(send_out, out_ref, part, parts + part)


def finish_kernel(lines_ref, contrast_ref, fh_ref, fl_ref, twiddle_ref, out_ref):
    devices, _, band, lanes = lines_ref.shape
    half_count = devices // 2
    half = half_count * band
    sides = []
    for side in range(2):
        some = slice(side * half_count, (side + 1) * half_count)
        stack = jnp.concatenate(
            [lines_ref[some, comp].reshape(half, lanes) for comp in range(2)], 0
        )
        result = product((fh_ref[...], fl_ref[...]), split(stack), ((1,), (0,)))
        sides.append((result[:half].T, result[half:].T))
    real_part, imag_part = butterfly_out(sides[0], sides[1], twiddle_ref)
    scale = contrast_ref[...] * (1.0 / (2 * half))
    out_ref[0] = real_part * scale
    out_ref[1] = imag_part * scale


def fast_body(wave_field, contrast, layer_of_plane, toeplitz_table, hankel_table, layer_rates):
    _, planes, rows, width_y = wave_field.shape
    lat_count, lay_count = lax.axis_size("lat"), lax.axis_size("lay")
    device_count = lat_count * lay_count
    width_x = rows * lat_count
    band = width_y // device_count
    parts = band // SUBLANES
    plane_total = planes * lay_count
    layer_count = layer_rates.shape[0]
    lines = planes * rows
    fh, fl, ih, il, twiddle = (jnp.asarray(t) for t in split_tables(width_y))
    smem = pl.BlockSpec(memory_space=pltpu.SMEM)
    vmem = pl.BlockSpec(memory_space=pltpu.VMEM)
    exchanged = (device_count, 2, band, lines)
    tile_all = (2, plane_total, SUBLANES, width_x)
    returned = pl.pallas_call(
        functools.partial(couple_kernel, lat_count, lay_count, planes, rows),
        out_shape=jax.ShapeDtypeStruct(exchanged, jnp.float32),
        in_specs=[smem] * 4 + [vmem] * 6,
        out_specs=vmem,
        scratch_shapes=[
            pltpu.VMEM(exchanged, jnp.float32),
            pltpu.VMEM(exchanged, jnp.float32),
            pltpu.VMEM(exchanged, jnp.float32),
            pltpu.VMEM(tile_all, jnp.float32),
            pltpu.VMEM(tile_all, jnp.float32),
            pltpu.VMEM(tile_all, jnp.float32),
            pltpu.VMEM((parts, layer_count, 2 * plane_total - 1, SUBLANES, width_x), jnp.float32),
            pltpu.SemaphoreType.DMA((2 * parts, device_count)),
            pltpu.SemaphoreType.DMA((2 * parts, device_count)),
        ],
        compiler_params=pltpu.CompilerParams(
            collective_id=0, has_side_effects=True, vmem_limit_bytes=60 * 1024 * 1024
        ),
        name="couple",
    )(
        layer_of_plane, layer_rates, toeplitz_table, hankel_table,
        wave_field.reshape(2, lines, width_y), fh, fl, ih, il, twiddle,
    )
    once = lambda shape: pl.BlockSpec(shape, lambda i: (0,) * len(shape))
    chunk = min(lines, LANES)
    result = pl.pallas_call(
        finish_kernel,
        grid=(lines // chunk,),
        out_shape=jax.ShapeDtypeStruct((2, lines, width_y), jnp.float32),
        in_specs=[
            pl.BlockSpec((device_count, 2, band, chunk), lambda i: (0, 0, 0, i)),
            pl.BlockSpec((chunk, width_y), lambda i: (i, 0)),
            once(fh.shape), once(fl.shape), once(twiddle.shape),
        ],
        out_specs=pl.BlockSpec((2, chunk, width_y), lambda i: (0, i, 0)),
        name="finish",
    )(returned, contrast.reshape(lines, width_y), fh, fl, twiddle)
    return result.reshape(wave_field.shape)


def body(wave_field, *others):
    _, planes, rows, width_y = wave_field.shape
    lat_count, lay_count = lax.axis_size("lat"), lax.axis_size("lay")
    device_count = lat_count * lay_count
    width_x = rows * lat_count
    fits = (
        2 * rows == LANES
        and planes % 2 == 0
        and width_x == width_y
        and width_y % (4 * LANES) == 0
        and width_y % (device_count * SUBLANES) == 0
        and device_count % 2 == 0
        and lat_count % 2 == 0
        and (planes * lay_count) % (LANES // SUBLANES) == 0
        and (planes * rows) % (2 * LANES) == 0
    )
    return (fast_body if fits else general_body)(wave_field, *others)


def solution(mesh):
    return jax.shard_map(
        body,
        mesh=mesh,
        in_specs=(P(None, "lay", "lat", None), P("lay", "lat", None), P(), P(), P(), P()),
        out_specs=P(None, "lay", "lat", None),
        check_vma=False,
    )
```

```python
import math

import functools

import jax
import jax.numpy as jnp
import numpy as np
from jax import lax
from jax.experimental import pallas as pl
from jax.experimental.pallas import tpu as pltpu
from jax.sharding import PartitionSpec as P

HIGHEST = lax.Precision.HIGHEST


def signed_of(index, amount):
    return jnp.where(index >= amount // 2, index - amount, index).astype(jnp.float32) / (amount / 2)


def phase_tables(rows, cols, amount, sign):
    index_row = lax.broadcasted_iota(jnp.int32, (rows, cols), 0)
    index_col = lax.broadcasted_iota(jnp.int32, (rows, cols), 1)
    angle = 2.0 * math.pi / amount * (index_row * index_col % amount).astype(jnp.float32)
    return (jnp.cos(angle), sign * jnp.sin(angle))


def complex_apply(real_part, imag_part, cos_table, sin_table, form):
    out_real = jnp.einsum(form, real_part, cos_table, precision=HIGHEST) - jnp.einsum(
        form, imag_part, sin_table, precision=HIGHEST
    )
    out_imag = jnp.einsum(form, real_part, sin_table, precision=HIGHEST) + jnp.einsum(
        form, imag_part, cos_table, precision=HIGHEST
    )
    return (out_real, out_imag)


def fourier_last(real_part, imag_part, sign, factor):
    amount = real_part.shape[-1]
    leading = real_part.shape[:-1]
    first = 1
    for divisor in range(1, math.isqrt(amount) + 1):
        if amount % divisor == 0:
            first = divisor
    second = amount // first
    flat_real = real_part.reshape(-1, second, first)
    flat_imag = imag_part.reshape(-1, second, first)
    cos_second, sin_second = phase_tables(second, second, second, sign)
    section_real, section_imag = complex_apply(
        flat_real, flat_imag, cos_second, sin_second, "pmn,mk->pkn"
    )
    twist_cos, twist_sin = phase_tables(second, first, amount, sign)
    turned_real = section_real * twist_cos - section_imag * twist_sin
    turned_imag = section_real * twist_sin + section_imag * twist_cos
    cos_first, sin_first = phase_tables(first, first, first, sign)
    final_real, final_imag = complex_apply(
        turned_real, turned_imag, cos_first, sin_first, "pkn,nj->pjk"
    )
    final_real = final_real.reshape(leading + (amount,)) * factor
    final_imag = final_imag.reshape(leading + (amount,)) * factor
    return (final_real, final_imag)


def pick_amplitudes(rows, index, width):
    positions = jnp.arange(width, dtype=jnp.int32)
    onehot = (index[:, :, None] == positions[None, None, :]).astype(jnp.float32)
    return jnp.einsum("pan,ain->pai", rows, onehot, precision=HIGHEST)


def general_body(wave_field, contrast, layer_of_plane, toeplitz_table, hankel_table, layer_rates):
    row_count = wave_field.shape[2]
    width_y = wave_field.shape[3]
    lat_count = lax.axis_size("lat")
    lay_count = lax.axis_size("lay")
    width_x = row_count * lat_count
    ky_band = width_y // lat_count
    table_width = toeplitz_table.shape[-1]
    plane_total = (table_width + 1) // 2
    layer_count = layer_rates.shape[0]
    spec_real, spec_imag = fourier_last(wave_field[0], wave_field[1], -1.0, 1.0)
    along_y = jnp.stack([spec_real, spec_imag], 2)
    freq_x = signed_of(jnp.arange(width_x, dtype=jnp.int32), width_x)
    ky_first = lax.axis_index("lat") * ky_band
    layer_ids = jnp.arange(layer_count, dtype=jnp.int32)

    def couple(z_out, z_in, source, ky_rows):
        onehot = (layer_of_plane[z_out][:, None] == layer_ids[None, :]).astype(jnp.float32)
        rate_out = jnp.dot(onehot, layer_rates, precision=HIGHEST)
        rows_toeplitz = jnp.einsum("al,pln->pan", onehot, toeplitz_table, precision=HIGHEST)
        rows_hankel = jnp.einsum("al,pln->pan", onehot, hankel_table, precision=HIGHEST)
        offset = z_out[:, None] - z_in[None, :]
        plane_sum = z_out[:, None] + z_in[None, :]
        amp_toeplitz = pick_amplitudes(rows_toeplitz, offset + plane_total - 1, table_width)
        amp_hankel = pick_amplitudes(rows_hankel, plane_sum, table_width)
        freq_y = signed_of(ky_rows, width_y)
        steepness = jnp.sqrt(1.0 + freq_y[:, None] ** 2 + freq_x[None, :] ** 2)
        scaled = rate_out[:, None, None, None] * steepness[None, None] / plane_total
        decay_toeplitz = jnp.exp(-scaled * jnp.abs(offset).astype(jnp.float32)[:, :, None, None])
        decay_hankel = jnp.exp(-scaled * (0.5 * plane_sum.astype(jnp.float32))[:, :, None, None])
        kern_real = (
            amp_toeplitz[0][:, :, None, None] * decay_toeplitz
            + amp_hankel[0][:, :, None, None] * decay_hankel
        )
        kern_imag = (
            amp_toeplitz[1][:, :, None, None] * decay_toeplitz
            + amp_hankel[1][:, :, None, None] * decay_hankel
        )
        real_src = source[None, :, 0]
        imag_src = source[None, :, 1]
        out_real = jnp.sum(kern_real * real_src - kern_imag * imag_src, axis=1)
        out_imag = jnp.sum(kern_real * imag_src + kern_imag * real_src, axis=1)
        return jnp.stack([out_real, out_imag], 1)

    narrow = ky_band // lay_count
    narrow_rows = ky_first + lax.axis_index("lay") * narrow + jnp.arange(narrow, dtype=jnp.int32)
    lines_in = lax.all_to_all(along_y, "lat", split_axis=3, concat_axis=1, tiled=True)
    line_real = jnp.transpose(lines_in[:, :, 0], (0, 2, 1))
    line_imag = jnp.transpose(lines_in[:, :, 1], (0, 2, 1))
    out_real, out_imag = fourier_last(line_real, line_imag, -1.0, 1.0)
    spectrum = jnp.stack([out_real, out_imag], 1)
    gathered = lax.all_to_all(spectrum, "lay", split_axis=2, concat_axis=0, tiled=True)
    all_planes = gathered.shape[0]
    every_plane = jnp.arange(all_planes, dtype=jnp.int32)
    block_size = math.gcd(all_planes, 8)

    def one_block(which):
        z_out = which * block_size + jnp.arange(block_size, dtype=jnp.int32)
        return couple(z_out, every_plane, gathered, narrow_rows)

    stacked = lax.map(one_block, jnp.arange(all_planes // block_size, dtype=jnp.int32))
    coupled = stacked.reshape(all_planes, 2, narrow_rows.shape[0], width_x)
    mixed = lax.all_to_all(coupled, "lay", split_axis=0, concat_axis=2, tiled=True)
    out_real, out_imag = fourier_last(mixed[:, 0], mixed[:, 1], 1.0, 1.0 / width_x)
    spatial_x = jnp.transpose(jnp.stack([out_real, out_imag], 1), (0, 3, 1, 2))
    lines = lax.all_to_all(spatial_x, "lat", split_axis=1, concat_axis=3, tiled=True)
    space_real, space_imag = fourier_last(lines[:, :, 0], lines[:, :, 1], 1.0, 1.0 / width_y)
    return jnp.stack([space_real, space_imag], 0) * contrast[None]


LANES = 128
SUBLANES = 8
MESH = pl.DeviceIdType.MESH


def split_tables(amount):
    half = amount // 2
    index = np.arange(half)
    angle = 2.0 * np.pi / half * (index[:, None] * index[None, :] % half)
    cos_part, sin_part = np.cos(angle), np.sin(angle)
    right = np.block([[cos_part, -sin_part], [sin_part, cos_part]]).astype(np.float32)
    high = right.astype(jnp.bfloat16)
    low = (right - high.astype(np.float32)).astype(jnp.bfloat16)
    turn = 2.0 * np.pi / amount * index
    twiddle = np.stack([np.cos(turn), np.sin(turn)]).astype(np.float32)
    return high, low, np.ascontiguousarray(high.T), np.ascontiguousarray(low.T), twiddle


def split(value):
    high = value.astype(jnp.bfloat16)
    return high, (value - high.astype(jnp.float32)).astype(jnp.bfloat16)


def product(left, right, contract):
    dot = functools.partial(
        lax.dot_general,
        dimension_numbers=(contract, ((), ())),
        preferred_element_type=jnp.float32,
    )
    return dot(left[0], right[0]) + (dot(left[1], right[0]) + dot(left[0], right[1]))


def swap_halves(first, second):
    low = lax.broadcasted_iota(jnp.int32, first.shape, first.ndim - 1) < LANES // 2
    one = jnp.where(low, first, pltpu.roll(second, LANES // 2, first.ndim - 1))
    two = jnp.where(low, pltpu.roll(first, LANES // 2, first.ndim - 1), second)
    return one, two


def butterfly_in(real_part, imag_part, twiddle):
    half = real_part.shape[-1] // 2
    cos_row, sin_row = twiddle[0:1, :], twiddle[1:2, :]
    even = (real_part[:, :half] + real_part[:, half:], imag_part[:, :half] + imag_part[:, half:])
    real_gap = real_part[:, :half] - real_part[:, half:]
    imag_gap = imag_part[:, :half] - imag_part[:, half:]
    odd = (
        real_gap * cos_row + imag_gap * sin_row,
        imag_gap * cos_row - real_gap * sin_row,
    )
    return even, odd


def butterfly_out(even, odd, twiddle):
    cos_row, sin_row = twiddle[0:1, :], twiddle[1:2, :]
    real_turn = odd[0] * cos_row - odd[1] * sin_row
    imag_turn = odd[0] * sin_row + odd[1] * cos_row
    real_part = jnp.concatenate([even[0] + real_turn, even[0] - real_turn], 1)
    imag_part = jnp.concatenate([even[1] + imag_turn, even[1] - imag_turn], 1)
    return real_part, imag_part


def couple_kernel(
    lat_count, lay_count, planes, rows,
    layer_ref, rate_ref, toeplitz_ref, hankel_ref,
    field_ref, fh_ref, fl_ref, ih_ref, il_ref, twiddle_ref,
    out_ref,
    send_in, recv_in, send_out, recv_out, field_x, spectrum, mixed, powers, even_y,
    send_sem, recv_sem,
):
    device_count = lat_count * lay_count
    my_lat, my_lay = lax.axis_index("lat"), lax.axis_index("lay")
    me = my_lat * lay_count + my_lay
    lines, width_y = field_ref.shape[1:]
    width_x = rows * lat_count
    half_y, half_x = width_y // 2, width_x // 2
    depth = half_y // device_count
    plane_total = planes * lay_count
    layer_count = rate_ref.shape[0]

    def partner(step):
        to_lat = (my_lat + step // lay_count) % lat_count
        to_lay = (my_lay + step % lay_count) % lay_count
        return to_lat, to_lay

    barrier = pltpu.get_barrier_semaphore()

    def greet(step, carry):
        pl.semaphore_signal(barrier, inc=1, device_id=partner(step), device_id_type=MESH)
        return carry

    lax.fori_loop(1, device_count, greet, 0)

    def exchange(source, target, part, phase, step):
        to_lat, to_lay = partner(step)
        return pltpu.make_async_remote_copy(
            src_ref=source.at[to_lat * lay_count + to_lay, part],
            dst_ref=target.at[me, part],
            send_sem=send_sem.at[phase, step],
            recv_sem=recv_sem.at[phase, step],
            device_id=(to_lat, to_lay),
            device_id_type=MESH,
        )

    def over_all(act):
        def one(step, carry):
            act(step)
            return carry

        lax.fori_loop(1, device_count, one, 0)

    chunk = min(lines, 2 * LANES)

    def transform_y(side):
        for start in range(0, lines, chunk):
            where = slice(start, start + chunk)
            pairs = butterfly_in(field_ref[0, where, :], field_ref[1, where, :], twiddle_ref)
            right = split(jnp.concatenate(pairs[side], 1))
            result = product((ih_ref[...], il_ref[...]), right, ((1,), (1,)))
            for comp in range(2):
                piece = result[comp * half_y:(comp + 1) * half_y]
                send_in[:, side, comp, :, where] = piece.reshape(device_count, depth, chunk)

    for side in range(2):
        transform_y(side)
        if side == 0:
            pl.semaphore_wait(barrier, device_count - 1)
        over_all(lambda step: exchange(send_in, recv_in, side, side, step).start())
        recv_in[me, side] = send_in[me, side]

    def signed(index, amount):
        index = jnp.where(index >= amount // 2, index - amount, index)
        return index.astype(jnp.float32) / (amount / 2)

    tile = (depth, width_x)
    place_x = lax.broadcasted_iota(jnp.int32, tile, 1)
    freq_x = signed(2 * (place_x % half_x) + place_x // half_x, width_x)
    for side in range(2):
        ky = 2 * (me * depth + lax.broadcasted_iota(jnp.int32, tile, 0)) + side
        freq_y = signed(ky, width_y)
        steepness = jnp.sqrt(1.0 + freq_x * freq_x + freq_y * freq_y)

        def one_layer(layer, carry):
            base = jnp.exp(steepness * (-rate_ref[layer] / (2 * plane_total)))

            def one_power(m, value):
                powers[side, layer, m] = value
                return value * base

            lax.fori_loop(0, 2 * plane_total - 1, one_power, jnp.ones(tile, jnp.float32))
            return carry

        lax.fori_loop(0, layer_count, one_layer, 0)

    def load_lines(side):
        def one_lay(lay, carry):
            for pair in range(planes // 2):
                lanes = slice(pair * LANES, (pair + 1) * LANES)
                for block in range(lat_count // 2):
                    first = recv_in[2 * block * lay_count + lay, side, :, :, lanes]
                    second = recv_in[(2 * block + 1) * lay_count + lay, side, :, :, lanes]
                    even, odd = swap_halves(first, second)
                    place = slice(block * LANES, (block + 1) * LANES)
                    field_x[:, lay * planes + 2 * pair, :, place] = even
                    field_x[:, lay * planes + 2 * pair + 1, :, place] = odd
            return carry

        lax.fori_loop(0, lay_count, one_lay, 0)

    group = min(plane_total, LANES // SUBLANES)

    def transform_x(step, carry):
        some = pl.ds(step * group, group)
        flat = (group * depth, width_x)
        pairs = butterfly_in(
            field_x[0, some].reshape(flat), field_x[1, some].reshape(flat), twiddle_ref
        )
        for side, pair in enumerate(pairs):
            left = split(jnp.concatenate(pair, 1))
            result = product(left, (fh_ref[...], fl_ref[...]), ((1,), (0,)))
            for comp in range(2):
                piece = result[:, comp * half_x:(comp + 1) * half_x]
                spectrum[comp, some, :, side * half_x:(side + 1) * half_x] = piece.reshape(
                    group, depth, half_x
                )
        return carry

    lays_step = 2 if lay_count % 2 == 0 else 1
    planes_step = planes * lays_step

    def lay_of(step, within):
        return (my_lay + 1 + step * lays_step + within) % lay_count

    def invert_x():
        sides = []
        for side in range(2):
            place = slice(side * half_x, (side + 1) * half_x)
            flat = (planes_step * depth, half_x)
            left = split(
                jnp.concatenate(
                    [mixed[comp, :, :, place].reshape(flat) for comp in range(2)], 1
                )
            )
            result = product(left, (ih_ref[...], il_ref[...]), ((1,), (0,)))
            sides.append((result[:, :half_x], result[:, half_x:]))
        real_part, imag_part = butterfly_out(sides[0], sides[1], twiddle_ref)
        full = (planes_step, depth, width_x)
        mixed[0] = (real_part * (1.0 / width_x)).reshape(full)
        mixed[1] = (imag_part * (1.0 / width_x)).reshape(full)

    def store_lines(side, lay, within):
        for pair in range(planes // 2):
            lanes = slice(pair * LANES, (pair + 1) * LANES)
            for block in range(lat_count // 2):
                place = slice(block * LANES, (block + 1) * LANES)
                even = mixed[:, within * planes + 2 * pair, :, place]
                odd = mixed[:, within * planes + 2 * pair + 1, :, place]
                first, second = swap_halves(even, odd)
                send_out[2 * block * lay_count + lay, side, :, :, lanes] = first
                send_out[(2 * block + 1) * lay_count + lay, side, :, :, lanes] = second

    def couple(side, lay, within):
        def one_plane(local, carry):
            plane = lay * planes + local
            layer = layer_ref[plane]
            real_sum = jnp.zeros(tile, jnp.float32)
            imag_sum = jnp.zeros(tile, jnp.float32)
            for source in range(plane_total):
                offset = plane - source
                direct = powers[side, layer, 2 * jnp.abs(offset)]
                mirror = powers[side, layer, plane + source]
                at = offset + plane_total - 1
                kern_real = (
                    toeplitz_ref[0, layer, at] * direct
                    + hankel_ref[0, layer, plane + source] * mirror
                )
                kern_imag = (
                    toeplitz_ref[1, layer, at] * direct
                    + hankel_ref[1, layer, plane + source] * mirror
                )
                real_src, imag_src = spectrum[0, source], spectrum[1, source]
                real_sum += kern_real * real_src - kern_imag * imag_src
                imag_sum += kern_real * imag_src + kern_imag * real_src
            mixed[0, within * planes + local] = real_sum
            mixed[1, within * planes + local] = imag_sum
            return carry

        lax.fori_loop(0, planes, one_plane, 0)

    for side in range(2):
        phase = 2 + side
        over_all(lambda step: exchange(send_in, recv_in, side, side, step).wait_recv())
        load_lines(side)
        lax.fori_loop(0, plane_total // group, transform_x, 0)

        def one_step(step, carry):
            for within in range(lays_step):
                couple(side, lay_of(step, within), within)
            invert_x()
            for within in range(lays_step):
                store_lines(side, lay_of(step, within), within)
            for within in range(lays_step):
                turn = (1 + step * lays_step + within) % lay_count

                def one_lat(lat_step, carry):
                    to = lat_step * lay_count + turn

                    @pl.when(to > 0)
                    def _():
                        exchange(send_out, recv_out, side, phase, to).start()

                    return carry

                lax.fori_loop(0, lat_count, one_lat, 0)
            return carry

        lax.fori_loop(0, lay_count // lays_step, one_step, 0)
        recv_out[me, side] = send_out[me, side]

    def invert_y(side, where):
        stack = jnp.concatenate(
            [recv_out[:, side, comp, :, where].reshape(half_y, LANES) for comp in range(2)], 0
        )
        result = product((fh_ref[...], fl_ref[...]), split(stack), ((1,), (0,)))
        return result[:half_y].T, result[half_y:].T

    over_all(lambda step: exchange(send_out, recv_out, 0, 2, step).wait_recv())
    for start in range(0, lines, LANES):
        where = slice(start, start + LANES)
        even_y[0, where], even_y[1, where] = invert_y(0, where)
    for side in range(2):
        over_all(lambda step: exchange(send_in, recv_in, side, side, step).wait_send())
    over_all(lambda step: exchange(send_out, recv_out, 0, 2, step).wait_send())
    over_all(lambda step: exchange(send_out, recv_out, 1, 3, step).wait_recv())
    for start in range(0, lines, LANES):
        where = slice(start, start + LANES)
        odd = invert_y(1, where)
        real_part, imag_part = butterfly_out((even_y[0, where], even_y[1, where]), odd, twiddle_ref)
        out_ref[0, where] = real_part * (1.0 / width_y)
        out_ref[1, where] = imag_part * (1.0 / width_y)
    over_all(lambda step: exchange(send_out, recv_out, 1, 3, step).wait_send())


def fast_body(wave_field, contrast, layer_of_plane, toeplitz_table, hankel_table, layer_rates):
    _, planes, rows, width_y = wave_field.shape
    lat_count, lay_count = lax.axis_size("lat"), lax.axis_size("lay")
    device_count = lat_count * lay_count
    width_x = rows * lat_count
    depth = width_y // (2 * device_count)
    plane_total = planes * lay_count
    layer_count = layer_rates.shape[0]
    lines = planes * rows
    fh, fl, ih, il, twiddle = (jnp.asarray(t) for t in split_tables(width_y))
    smem = pl.BlockSpec(memory_space=pltpu.SMEM)
    vmem = pl.BlockSpec(memory_space=pltpu.VMEM)
    exchanged = (device_count, 2, 2, depth, lines)
    tile_all = (2, plane_total, depth, width_x)
    lays_step = 2 if lay_count % 2 == 0 else 1
    space = pl.pallas_call(
        functools.partial(couple_kernel, lat_count, lay_count, planes, rows),
        out_shape=jax.ShapeDtypeStruct((2, lines, width_y), jnp.float32),
        in_specs=[smem] * 4 + [vmem] * 6,
        out_specs=vmem,
        scratch_shapes=[
            pltpu.VMEM(exchanged, jnp.float32),
            pltpu.VMEM(exchanged, jnp.float32),
            pltpu.VMEM(exchanged, jnp.float32),
            pltpu.VMEM(exchanged, jnp.float32),
            pltpu.VMEM(tile_all, jnp.float32),
            pltpu.VMEM(tile_all, jnp.float32),
            pltpu.VMEM((2, planes * lays_step, depth, width_x), jnp.float32),
            pltpu.VMEM((2, layer_count, 2 * plane_total - 1, depth, width_x), jnp.float32),
            pltpu.VMEM((2, lines, width_y // 2), jnp.float32),
            pltpu.SemaphoreType.DMA((4, device_count)),
            pltpu.SemaphoreType.DMA((4, device_count)),
        ],
        compiler_params=pltpu.CompilerParams(
            collective_id=0, has_side_effects=True, vmem_limit_bytes=60 * 1024 * 1024
        ),
        name="couple",
    )(
        layer_of_plane, layer_rates, toeplitz_table, hankel_table,
        wave_field.reshape(2, lines, width_y), fh, fl, ih, il, twiddle,
    )
    return space.reshape(wave_field.shape) * contrast[None]


def body(wave_field, *others):
    _, planes, rows, width_y = wave_field.shape
    lat_count, lay_count = lax.axis_size("lat"), lax.axis_size("lay")
    device_count = lat_count * lay_count
    width_x = rows * lat_count
    fits = (
        2 * rows == LANES
        and planes % 2 == 0
        and width_x == width_y
        and width_y % (4 * LANES) == 0
        and width_y == 2 * device_count * SUBLANES
        and device_count % 2 == 0
        and lat_count % 2 == 0
        and (planes * lay_count) % (LANES // SUBLANES) == 0
        and (planes * rows) % (2 * LANES) == 0
    )
    return (fast_body if fits else general_body)(wave_field, *others)


def solution(mesh):
    return jax.shard_map(
        body,
        mesh=mesh,
        in_specs=(P(None, "lay", "lat", None), P("lay", "lat", None), P(), P(), P(), P()),
        out_specs=P(None, "lay", "lat", None),
        check_vma=False,
    )
```

```python
import math

import functools

import jax
import jax.numpy as jnp
import numpy as np
from jax import lax
from jax.experimental import pallas as pl
from jax.experimental.pallas import tpu as pltpu
from jax.sharding import PartitionSpec as P

HIGHEST = lax.Precision.HIGHEST


def signed_of(index, amount):
    return jnp.where(index >= amount // 2, index - amount, index).astype(jnp.float32) / (amount / 2)


def phase_tables(rows, cols, amount, sign):
    index_row = lax.broadcasted_iota(jnp.int32, (rows, cols), 0)
    index_col = lax.broadcasted_iota(jnp.int32, (rows, cols), 1)
    angle = 2.0 * math.pi / amount * (index_row * index_col % amount).astype(jnp.float32)
    return (jnp.cos(angle), sign * jnp.sin(angle))


def complex_apply(real_part, imag_part, cos_table, sin_table, form):
    out_real = jnp.einsum(form, real_part, cos_table, precision=HIGHEST) - jnp.einsum(
        form, imag_part, sin_table, precision=HIGHEST
    )
    out_imag = jnp.einsum(form, real_part, sin_table, precision=HIGHEST) + jnp.einsum(
        form, imag_part, cos_table, precision=HIGHEST
    )
    return (out_real, out_imag)


def fourier_last(real_part, imag_part, sign, factor):
    amount = real_part.shape[-1]
    leading = real_part.shape[:-1]
    first = 1
    for divisor in range(1, math.isqrt(amount) + 1):
        if amount % divisor == 0:
            first = divisor
    second = amount // first
    flat_real = real_part.reshape(-1, second, first)
    flat_imag = imag_part.reshape(-1, second, first)
    cos_second, sin_second = phase_tables(second, second, second, sign)
    section_real, section_imag = complex_apply(
        flat_real, flat_imag, cos_second, sin_second, "pmn,mk->pkn"
    )
    twist_cos, twist_sin = phase_tables(second, first, amount, sign)
    turned_real = section_real * twist_cos - section_imag * twist_sin
    turned_imag = section_real * twist_sin + section_imag * twist_cos
    cos_first, sin_first = phase_tables(first, first, first, sign)
    final_real, final_imag = complex_apply(
        turned_real, turned_imag, cos_first, sin_first, "pkn,nj->pjk"
    )
    final_real = final_real.reshape(leading + (amount,)) * factor
    final_imag = final_imag.reshape(leading + (amount,)) * factor
    return (final_real, final_imag)


def pick_amplitudes(rows, index, width):
    positions = jnp.arange(width, dtype=jnp.int32)
    onehot = (index[:, :, None] == positions[None, None, :]).astype(jnp.float32)
    return jnp.einsum("pan,ain->pai", rows, onehot, precision=HIGHEST)


def general_body(wave_field, contrast, layer_of_plane, toeplitz_table, hankel_table, layer_rates):
    row_count = wave_field.shape[2]
    width_y = wave_field.shape[3]
    lat_count = lax.axis_size("lat")
    lay_count = lax.axis_size("lay")
    width_x = row_count * lat_count
    ky_band = width_y // lat_count
    table_width = toeplitz_table.shape[-1]
    plane_total = (table_width + 1) // 2
    layer_count = layer_rates.shape[0]
    spec_real, spec_imag = fourier_last(wave_field[0], wave_field[1], -1.0, 1.0)
    along_y = jnp.stack([spec_real, spec_imag], 2)
    freq_x = signed_of(jnp.arange(width_x, dtype=jnp.int32), width_x)
    ky_first = lax.axis_index("lat") * ky_band
    layer_ids = jnp.arange(layer_count, dtype=jnp.int32)

    def couple(z_out, z_in, source, ky_rows):
        onehot = (layer_of_plane[z_out][:, None] == layer_ids[None, :]).astype(jnp.float32)
        rate_out = jnp.dot(onehot, layer_rates, precision=HIGHEST)
        rows_toeplitz = jnp.einsum("al,pln->pan", onehot, toeplitz_table, precision=HIGHEST)
        rows_hankel = jnp.einsum("al,pln->pan", onehot, hankel_table, precision=HIGHEST)
        offset = z_out[:, None] - z_in[None, :]
        plane_sum = z_out[:, None] + z_in[None, :]
        amp_toeplitz = pick_amplitudes(rows_toeplitz, offset + plane_total - 1, table_width)
        amp_hankel = pick_amplitudes(rows_hankel, plane_sum, table_width)
        freq_y = signed_of(ky_rows, width_y)
        steepness = jnp.sqrt(1.0 + freq_y[:, None] ** 2 + freq_x[None, :] ** 2)
        scaled = rate_out[:, None, None, None] * steepness[None, None] / plane_total
        decay_toeplitz = jnp.exp(-scaled * jnp.abs(offset).astype(jnp.float32)[:, :, None, None])
        decay_hankel = jnp.exp(-scaled * (0.5 * plane_sum.astype(jnp.float32))[:, :, None, None])
        kern_real = (
            amp_toeplitz[0][:, :, None, None] * decay_toeplitz
            + amp_hankel[0][:, :, None, None] * decay_hankel
        )
        kern_imag = (
            amp_toeplitz[1][:, :, None, None] * decay_toeplitz
            + amp_hankel[1][:, :, None, None] * decay_hankel
        )
        real_src = source[None, :, 0]
        imag_src = source[None, :, 1]
        out_real = jnp.sum(kern_real * real_src - kern_imag * imag_src, axis=1)
        out_imag = jnp.sum(kern_real * imag_src + kern_imag * real_src, axis=1)
        return jnp.stack([out_real, out_imag], 1)

    narrow = ky_band // lay_count
    narrow_rows = ky_first + lax.axis_index("lay") * narrow + jnp.arange(narrow, dtype=jnp.int32)
    lines_in = lax.all_to_all(along_y, "lat", split_axis=3, concat_axis=1, tiled=True)
    line_real = jnp.transpose(lines_in[:, :, 0], (0, 2, 1))
    line_imag = jnp.transpose(lines_in[:, :, 1], (0, 2, 1))
    out_real, out_imag = fourier_last(line_real, line_imag, -1.0, 1.0)
    spectrum = jnp.stack([out_real, out_imag], 1)
    gathered = lax.all_to_all(spectrum, "lay", split_axis=2, concat_axis=0, tiled=True)
    all_planes = gathered.shape[0]
    every_plane = jnp.arange(all_planes, dtype=jnp.int32)
    block_size = math.gcd(all_planes, 8)

    def one_block(which):
        z_out = which * block_size + jnp.arange(block_size, dtype=jnp.int32)
        return couple(z_out, every_plane, gathered, narrow_rows)

    stacked = lax.map(one_block, jnp.arange(all_planes // block_size, dtype=jnp.int32))
    coupled = stacked.reshape(all_planes, 2, narrow_rows.shape[0], width_x)
    mixed = lax.all_to_all(coupled, "lay", split_axis=0, concat_axis=2, tiled=True)
    out_real, out_imag = fourier_last(mixed[:, 0], mixed[:, 1], 1.0, 1.0 / width_x)
    spatial_x = jnp.transpose(jnp.stack([out_real, out_imag], 1), (0, 3, 1, 2))
    lines = lax.all_to_all(spatial_x, "lat", split_axis=1, concat_axis=3, tiled=True)
    space_real, space_imag = fourier_last(lines[:, :, 0], lines[:, :, 1], 1.0, 1.0 / width_y)
    return jnp.stack([space_real, space_imag], 0) * contrast[None]


LANES = 128
SUBLANES = 8
MESH = pl.DeviceIdType.MESH


def split_tables(amount):
    half = amount // 2
    index = np.arange(half)
    angle = 2.0 * np.pi / half * (index[:, None] * index[None, :] % half)
    cos_part, sin_part = np.cos(angle), np.sin(angle)
    right = np.block([[cos_part, -sin_part], [sin_part, cos_part]]).astype(np.float32)
    high = right.astype(jnp.bfloat16)
    low = (right - high.astype(np.float32)).astype(jnp.bfloat16)
    turn = 2.0 * np.pi / amount * index
    twiddle = np.stack([np.cos(turn), np.sin(turn)]).astype(np.float32)
    return high, low, np.ascontiguousarray(high.T), np.ascontiguousarray(low.T), twiddle


def split(value):
    high = value.astype(jnp.bfloat16)
    return high, (value - high.astype(jnp.float32)).astype(jnp.bfloat16)


def product(left, right, contract):
    dot = functools.partial(
        lax.dot_general,
        dimension_numbers=(contract, ((), ())),
        preferred_element_type=jnp.float32,
    )
    return dot(left[0], right[0]) + (dot(left[1], right[0]) + dot(left[0], right[1]))


def swap_halves(first, second):
    low = lax.broadcasted_iota(jnp.int32, first.shape, first.ndim - 1) < LANES // 2
    one = jnp.where(low, first, pltpu.roll(second, LANES // 2, first.ndim - 1))
    two = jnp.where(low, pltpu.roll(first, LANES // 2, first.ndim - 1), second)
    return one, two


def butterfly_in(real_part, imag_part, twiddle):
    half = real_part.shape[-1] // 2
    cos_row, sin_row = twiddle[0:1, :], twiddle[1:2, :]
    even = (real_part[:, :half] + real_part[:, half:], imag_part[:, :half] + imag_part[:, half:])
    real_gap = real_part[:, :half] - real_part[:, half:]
    imag_gap = imag_part[:, :half] - imag_part[:, half:]
    odd = (
        real_gap * cos_row + imag_gap * sin_row,
        imag_gap * cos_row - real_gap * sin_row,
    )
    return even, odd


def butterfly_out(even, odd, twiddle):
    cos_row, sin_row = twiddle[0:1, :], twiddle[1:2, :]
    real_turn = odd[0] * cos_row - odd[1] * sin_row
    imag_turn = odd[0] * sin_row + odd[1] * cos_row
    real_part = jnp.concatenate([even[0] + real_turn, even[0] - real_turn], 1)
    imag_part = jnp.concatenate([even[1] + imag_turn, even[1] - imag_turn], 1)
    return real_part, imag_part


def couple_kernel(
    lat_count, lay_count, planes, rows,
    layer_ref, rate_ref, toeplitz_ref, hankel_ref,
    field_any, fh_any, fl_any, ih_any, il_any, twiddle_ref,
    out_any,
    send_in, recv_in, send_out, recv_out, field_x, spectrum, mixed, powers, even_y,
    field_ref, fh_ref, fl_ref, ih_ref, il_ref, out_ref,
    send_sem, recv_sem, load_sem, store_sem,
):
    device_count = lat_count * lay_count
    my_lat, my_lay = lax.axis_index("lat"), lax.axis_index("lay")
    me = my_lat * lay_count + my_lay
    lines, width_y = field_ref.shape[1:]
    width_x = rows * lat_count
    half_y, half_x = width_y // 2, width_x // 2
    depth = half_y // device_count
    plane_total = planes * lay_count
    layer_count = rate_ref.shape[0]

    own_step = 0

    def partner(step):
        lat_step = step // lay_count
        to_lat = (my_lat + lat_step) % lat_count
        to_lay = (my_lay + step % lay_count) % lay_count
        return to_lat, to_lay

    def over_all(act):
        def one(step, carry):
            act(step)
            return carry

        lax.fori_loop(0, own_step, one, 0)
        lax.fori_loop(own_step + 1, device_count, one, 0)

    chunk = min(lines, 2 * LANES)
    chunks = lines // chunk
    loads = [
        pltpu.make_async_copy(
            field_any.at[:, pl.ds(i * chunk, chunk)],
            field_ref.at[:, pl.ds(i * chunk, chunk)],
            load_sem.at[i],
        )
        for i in range(chunks)
    ] + [
        pltpu.make_async_copy(source, target, load_sem.at[chunks + i])
        for i, (source, target) in enumerate(
            [(ih_any, ih_ref), (il_any, il_ref), (fh_any, fh_ref), (fl_any, fl_ref)]
        )
    ]
    for i in [0, chunks, chunks + 1, *range(1, chunks), chunks + 2, chunks + 3]:
        loads[i].start()

    barrier = pltpu.get_barrier_semaphore()

    over_all(
        lambda step: pl.semaphore_signal(
            barrier, inc=1, device_id=partner(step), device_id_type=MESH
        )
    )

    def exchange(source, target, part, phase, step):
        to_lat, to_lay = partner(step)
        return pltpu.make_async_remote_copy(
            src_ref=source.at[to_lat * lay_count + to_lay, part],
            dst_ref=target.at[me, part],
            send_sem=send_sem.at[phase, step],
            recv_sem=recv_sem.at[phase, step],
            device_id=(to_lat, to_lay),
            device_id_type=MESH,
        )

    loads[chunks].wait()
    loads[chunks + 1].wait()

    def transform_y(side):
        for start in range(0, lines, chunk):
            where = slice(start, start + chunk)
            if side == 0:
                loads[start // chunk].wait()
            pairs = butterfly_in(field_ref[0, where, :], field_ref[1, where, :], twiddle_ref)
            right = split(jnp.concatenate(pairs[side], 1))
            result = product((ih_ref[...], il_ref[...]), right, ((1,), (1,)))
            for comp in range(2):
                piece = result[comp * half_y:(comp + 1) * half_y]
                send_in[:, side, comp, :, where] = piece.reshape(device_count, depth, chunk)

    for side in range(2):
        transform_y(side)
        if side == 0:
            pl.semaphore_wait(barrier, device_count - 1)
        over_all(lambda step: exchange(send_in, recv_in, side, side, step).start())
        recv_in[me, side] = send_in[me, side]

    def signed(index, amount):
        index = jnp.where(index >= amount // 2, index - amount, index)
        return index.astype(jnp.float32) / (amount / 2)

    tile = (depth, width_x)
    place_x = lax.broadcasted_iota(jnp.int32, tile, 1)
    freq_x = signed(2 * (place_x % half_x) + place_x // half_x, width_x)
    for side in range(2):
        ky = 2 * (me * depth + lax.broadcasted_iota(jnp.int32, tile, 0)) + side
        freq_y = signed(ky, width_y)
        steepness = jnp.sqrt(1.0 + freq_x * freq_x + freq_y * freq_y)

        def one_layer(layer, carry):
            base = jnp.exp(steepness * (-rate_ref[layer] / (2 * plane_total)))

            def one_power(m, value):
                powers[side, layer, m] = value
                return value * base

            lax.fori_loop(0, 2 * plane_total - 1, one_power, jnp.ones(tile, jnp.float32))
            return carry

        lax.fori_loop(0, layer_count, one_layer, 0)

    loads[chunks + 2].wait()
    loads[chunks + 3].wait()

    def load_lines(side):
        def one_lay(lay, carry):
            for pair in range(planes // 2):
                lanes = slice(pair * LANES, (pair + 1) * LANES)
                for block in range(lat_count // 2):
                    first = recv_in[2 * block * lay_count + lay, side, :, :, lanes]
                    second = recv_in[(2 * block + 1) * lay_count + lay, side, :, :, lanes]
                    even, odd = swap_halves(first, second)
                    place = slice(block * LANES, (block + 1) * LANES)
                    field_x[:, lay * planes + 2 * pair, :, place] = even
                    field_x[:, lay * planes + 2 * pair + 1, :, place] = odd
            return carry

        lax.fori_loop(0, lay_count, one_lay, 0)

    group = min(plane_total, LANES // SUBLANES)

    def transform_x(step, carry):
        some = pl.ds(step * group, group)
        flat = (group * depth, width_x)
        pairs = butterfly_in(
            field_x[0, some].reshape(flat), field_x[1, some].reshape(flat), twiddle_ref
        )
        for side, pair in enumerate(pairs):
            left = split(jnp.concatenate(pair, 1))
            result = product(left, (fh_ref[...], fl_ref[...]), ((1,), (0,)))
            for comp in range(2):
                piece = result[:, comp * half_x:(comp + 1) * half_x]
                spectrum[comp, some, :, side * half_x:(side + 1) * half_x] = piece.reshape(
                    group, depth, half_x
                )
        return carry

    lays_step = 2 if lay_count % 2 == 0 else 1
    planes_step = planes * lays_step

    def lay_of(step, within):
        return (my_lay + 1 + step * lays_step + within) % lay_count

    def invert_x():
        sides = []
        for side in range(2):
            place = slice(side * half_x, (side + 1) * half_x)
            flat = (planes_step * depth, half_x)
            left = split(
                jnp.concatenate(
                    [mixed[comp, :, :, place].reshape(flat) for comp in range(2)], 1
                )
            )
            result = product(left, (ih_ref[...], il_ref[...]), ((1,), (0,)))
            sides.append((result[:, :half_x], result[:, half_x:]))
        real_part, imag_part = butterfly_out(sides[0], sides[1], twiddle_ref)
        full = (planes_step, depth, width_x)
        mixed[0] = (real_part * (1.0 / width_x)).reshape(full)
        mixed[1] = (imag_part * (1.0 / width_x)).reshape(full)

    def store_lines(side, lay, within):
        for pair in range(planes // 2):
            lanes = slice(pair * LANES, (pair + 1) * LANES)
            for block in range(lat_count // 2):
                place = slice(block * LANES, (block + 1) * LANES)
                even = mixed[:, within * planes + 2 * pair, :, place]
                odd = mixed[:, within * planes + 2 * pair + 1, :, place]
                first, second = swap_halves(even, odd)
                send_out[2 * block * lay_count + lay, side, :, :, lanes] = first
                send_out[(2 * block + 1) * lay_count + lay, side, :, :, lanes] = second

    def couple(side, lay, within):
        def one_plane(local, carry):
            plane = lay * planes + local
            layer = layer_ref[plane]
            real_sum = jnp.zeros(tile, jnp.float32)
            imag_sum = jnp.zeros(tile, jnp.float32)
            for source in range(plane_total):
                offset = plane - source
                direct = powers[side, layer, 2 * jnp.abs(offset)]
                mirror = powers[side, layer, plane + source]
                at = offset + plane_total - 1
                kern_real = (
                    toeplitz_ref[0, layer, at] * direct
                    + hankel_ref[0, layer, plane + source] * mirror
                )
                kern_imag = (
                    toeplitz_ref[1, layer, at] * direct
                    + hankel_ref[1, layer, plane + source] * mirror
                )
                real_src, imag_src = spectrum[0, source], spectrum[1, source]
                real_sum += kern_real * real_src - kern_imag * imag_src
                imag_sum += kern_real * imag_src + kern_imag * real_src
            mixed[0, within * planes + local] = real_sum
            mixed[1, within * planes + local] = imag_sum
            return carry

        lax.fori_loop(0, planes, one_plane, 0)

    for side in range(2):
        phase = 2 + side
        over_all(lambda step: exchange(send_in, recv_in, side, side, step).wait_recv())
        load_lines(side)
        lax.fori_loop(0, plane_total // group, transform_x, 0)

        def one_step(step, carry):
            for within in range(lays_step):
                couple(side, lay_of(step, within), within)
            invert_x()
            for within in range(lays_step):
                store_lines(side, lay_of(step, within), within)
            for within in range(lays_step):
                turn = (1 + step * lays_step + within) % lay_count

                def one_lat(lat_step, carry):
                    to = lat_step * lay_count + turn

                    @pl.when(to != own_step)
                    def _():
                        exchange(send_out, recv_out, side, phase, to).start()

                    return carry

                lax.fori_loop(0, lat_count, one_lat, 0)
            return carry

        lax.fori_loop(0, lay_count // lays_step, one_step, 0)
        recv_out[me, side] = send_out[me, side]

    def invert_y(side, where):
        stack = jnp.concatenate(
            [recv_out[:, side, comp, :, where].reshape(half_y, LANES) for comp in range(2)], 0
        )
        result = product((fh_ref[...], fl_ref[...]), split(stack), ((1,), (0,)))
        return result[:half_y].T, result[half_y:].T

    over_all(lambda step: exchange(send_out, recv_out, 0, 2, step).wait_recv())
    for start in range(0, lines, LANES):
        where = slice(start, start + LANES)
        even_y[0, where], even_y[1, where] = invert_y(0, where)
    for side in range(2):
        over_all(lambda step: exchange(send_in, recv_in, side, side, step).wait_send())
    over_all(lambda step: exchange(send_out, recv_out, 0, 2, step).wait_send())
    over_all(lambda step: exchange(send_out, recv_out, 1, 3, step).wait_recv())
    stores = []
    for start in range(0, lines, LANES):
        where = pl.ds(start, LANES)
        odd = invert_y(1, where)
        real_part, imag_part = butterfly_out((even_y[0, where], even_y[1, where]), odd, twiddle_ref)
        out_ref[0, where] = real_part * (1.0 / width_y)
        out_ref[1, where] = imag_part * (1.0 / width_y)
        stores.append(
            pltpu.make_async_copy(
                out_ref.at[:, where], out_any.at[:, where], store_sem.at[start // LANES]
            )
        )
        stores[-1].start()
    for store in stores:
        store.wait()
    over_all(lambda step: exchange(send_out, recv_out, 1, 3, step).wait_send())


def fast_body(wave_field, contrast, layer_of_plane, toeplitz_table, hankel_table, layer_rates):
    _, planes, rows, width_y = wave_field.shape
    lat_count, lay_count = lax.axis_size("lat"), lax.axis_size("lay")
    device_count = lat_count * lay_count
    width_x = rows * lat_count
    depth = width_y // (2 * device_count)
    plane_total = planes * lay_count
    layer_count = layer_rates.shape[0]
    lines = planes * rows
    fh, fl, ih, il, twiddle = (jnp.asarray(t) for t in split_tables(width_y))
    smem = pl.BlockSpec(memory_space=pltpu.SMEM)
    vmem = pl.BlockSpec(memory_space=pltpu.VMEM)
    anywhere = pl.BlockSpec(memory_space=pl.ANY)
    exchanged = (device_count, 2, 2, depth, lines)
    tile_all = (2, plane_total, depth, width_x)
    lays_step = 2 if lay_count % 2 == 0 else 1
    space = pl.pallas_call(
        functools.partial(couple_kernel, lat_count, lay_count, planes, rows),
        out_shape=jax.ShapeDtypeStruct((2, lines, width_y), jnp.float32),
        in_specs=[smem] * 4 + [anywhere] * 5 + [vmem],
        out_specs=anywhere,
        scratch_shapes=[
            pltpu.VMEM(exchanged, jnp.float32),
            pltpu.VMEM(exchanged, jnp.float32),
            pltpu.VMEM(exchanged, jnp.float32),
            pltpu.VMEM(exchanged, jnp.float32),
            pltpu.VMEM(tile_all, jnp.float32),
            pltpu.VMEM(tile_all, jnp.float32),
            pltpu.VMEM((2, planes * lays_step, depth, width_x), jnp.float32),
            pltpu.VMEM((2, layer_count, 2 * plane_total - 1, depth, width_x), jnp.float32),
            pltpu.VMEM((2, lines, width_y // 2), jnp.float32),
            pltpu.VMEM((2, lines, width_y), jnp.float32),
            pltpu.VMEM(fh.shape, fh.dtype),
            pltpu.VMEM(fl.shape, fl.dtype),
            pltpu.VMEM(ih.shape, ih.dtype),
            pltpu.VMEM(il.shape, il.dtype),
            pltpu.VMEM((2, lines, width_y), jnp.float32),
            pltpu.SemaphoreType.DMA((4, device_count)),
            pltpu.SemaphoreType.DMA((4, device_count)),
            pltpu.SemaphoreType.DMA((lines // min(lines, 2 * LANES) + 4,)),
            pltpu.SemaphoreType.DMA((lines // LANES,)),
        ],
        compiler_params=pltpu.CompilerParams(
            collective_id=0, has_side_effects=True, vmem_limit_bytes=60 * 1024 * 1024
        ),
        name="couple",
    )(
        layer_of_plane, layer_rates, toeplitz_table, hankel_table,
        wave_field.reshape(2, lines, width_y), fh, fl, ih, il, twiddle,
    )
    return space.reshape(wave_field.shape) * contrast[None]


def body(wave_field, *others):
    _, planes, rows, width_y = wave_field.shape
    lat_count, lay_count = lax.axis_size("lat"), lax.axis_size("lay")
    device_count = lat_count * lay_count
    width_x = rows * lat_count
    fits = (
        2 * rows == LANES
        and planes % 2 == 0
        and width_x == width_y
        and width_y % (4 * LANES) == 0
        and width_y == 2 * device_count * SUBLANES
        and device_count % 2 == 0
        and lat_count % 2 == 0
        and (planes * lay_count) % (LANES // SUBLANES) == 0
        and (planes * rows) % (2 * LANES) == 0
    )
    return (fast_body if fits else general_body)(wave_field, *others)


def solution(mesh):
    return jax.shard_map(
        body,
        mesh=mesh,
        in_specs=(P(None, "lay", "lat", None), P("lay", "lat", None), P(), P(), P(), P()),
        out_specs=P(None, "lay", "lat", None),
        check_vma=False,
    )
```
